32 devices in a mesh: dp: 8 (over y, x, core), fsdp: 4 (over z).
Axes of the slice: x: 2, y: 2, z: 4, core: 2. Of those that a mesh axis runs over, the one named last changes fastest.
Arguments:
- img_emb: bfloat16 [1024, 1024], P(('dp', 'fsdp')), may hold values from -0.25 to 0.25
- txt_emb: bfloat16 [1024, 1024], P(('dp', 'fsdp')), may hold values from -0.25 to 0.25
- img_ids: int32 [1024], P(('dp', 'fsdp')), may hold values from 0 to 1023
- txt_ids: int32 [1024], P(('dp', 'fsdp')), may hold values from 0 to 1023
- temp_log: float32 [1], replicated, may hold values from 1.5 to 2.5
- logit_bias: float32 [1], replicated, may hold values from -6 to -2
- block_in: bfloat16 [2048, 3072], P(('dp', 'fsdp')), may hold values from -6 to 6
- dw_kernel: float32 [49, 3072], replicated, may hold values from -0.875 to 0.875
- ln_gain: float32 [3072], replicated, may hold values from 0.5 to 1.5
- ln_bias: float32 [3072], replicated, may hold values from -3 to 3
- w_up: bfloat16 [3072, 6144], P(None, 'fsdp'), may hold values from -0.109375 to 0.109375
- w_down: bfloat16 [6144, 3072], P('fsdp'), may hold values from -0.078125 to 0.078125
- layer_scale: float32 [3072], replicated, may hold values from 0.1 to 1
- head_gain: float32 [3072], replicated, may hold values from 0.5 to 1.5
- head_bias: float32 [3072], replicated, may hold values from -3 to 3
- w_proj: bfloat16 [3072, 1024], replicated, may hold values from -0.109375 to 0.109375
Outputs:
- img_grad: float32 [1024, 1024], P(('dp', 'fsdp'))
- txt_grad: float32 [1024, 1024], P(('dp', 'fsdp'))
- w_up_grad: float32 [3072, 6144], P('dp', 'fsdp')
- w_down_grad: float32 [6144, 3072], P('fsdp', 'dp')
The draws below stay inside these ranges and needn't reach their ends.
All inputs are finite; a program needn't handle non-finite values.
Results may differ from the reference program's by a relative error of at most 0.02.
Values may be sent and summed in bfloat16 or wider, within the bound.
A program may use at most 128 MiB of HBM per device.

```python
import math
import jax
import jax.numpy as jnp
from jax import lax

WIDTH = 3072
HIDDEN_SIZE = 6144
EMBED = 1024
KERNEL = 7
SIDE = 8
PAIR_DEV = 32
PAIRS = 1024
IMAGE_ROWS = 2048
N_DP = 8
N_FSDP = 4


def set_ends(result, rng, least, top_value):
    shape = result.shape
    spot = [jax.random.randint(jax.random.fold_in(rng, axis), (), 0, shape[axis]) for axis in range(len(shape))]
    result = result.at[tuple(spot)].set(least)
    longest = shape.index(max(shape))
    spot[longest] = (spot[longest] + 1) % shape[longest]
    return result.at[tuple(spot)].set(top_value)


def block_levels(rng, dims, pieces, low, top_value):
    gain, own = 1.0, jax.random.fold_in(rng, 6)
    for dim, blocks in pieces:
        heights = jnp.exp(jax.random.uniform(jax.random.fold_in(own, dim), (blocks,), jnp.float32, low / len(pieces), top_value / len(pieces)))
        gain = gain * jnp.repeat(heights, dims[dim] // blocks).reshape([-1 if axis == dim else 1 for axis in range(len(dims))])
    return gain


def scatter_about(rng, dims, deviation, limit, cuts=(), held_as=jnp.bfloat16):
    values = deviation * jax.random.normal(rng, dims, jnp.float32)
    if cuts:
        values = values * block_levels(rng, dims, cuts, -0.22, 0.18)
    return jnp.clip(values, -limit, limit).astype(held_as)


def setup_inputs(seed: int = 0) -> dict:
    seeds = jax.random.split(jax.random.key(seed), 17)
    return {
        "img_emb": scatter_about(seeds[0], (PAIRS, EMBED), 0.03125, 0.25, ((0, 32),)),
        "txt_emb": scatter_about(seeds[1], (PAIRS, EMBED), 0.03125, 0.25, ((0, 32),)),
        "img_ids": set_ends(jax.random.randint(seeds[2], (PAIRS,), 0, PAIRS), jax.random.fold_in(seeds[2], 1), 0, PAIRS - 1).astype(jnp.int32),
        "txt_ids": set_ends(jax.random.randint(seeds[3], (PAIRS,), 0, PAIRS), jax.random.fold_in(seeds[3], 1), 0, PAIRS - 1).astype(jnp.int32),
        "temp_log": jnp.clip(jax.random.uniform(seeds[4], (1,), jnp.float32, 1.5, 2.5), 1.5, 2.5),
        "logit_bias": jnp.clip(jax.random.uniform(seeds[5], (1,), jnp.float32, -6.0, -2.0), -6.0, -2.0),
        "block_in": scatter_about(seeds[6], (IMAGE_ROWS, WIDTH), 1.0, 6.0, ((0, 32),)),
        "dw_kernel": scatter_about(seeds[7], (KERNEL * KERNEL, WIDTH), (KERNEL * KERNEL) ** -0.5, 0.875, (), jnp.float32),
        "ln_gain": jnp.clip(1.0 + 0.1 * jax.random.normal(seeds[8], (WIDTH,), jnp.float32), 0.5, 1.5),
        "ln_bias": scatter_about(seeds[9], (WIDTH,), 0.5, 3.0, (), jnp.float32),
        "w_up": scatter_about(seeds[10], (WIDTH, HIDDEN_SIZE), WIDTH ** -0.5, 0.109375, ((1, 4),)),
        "w_down": scatter_about(seeds[11], (HIDDEN_SIZE, WIDTH), HIDDEN_SIZE ** -0.5, 0.078125, ((0, 4),)),
        "layer_scale": jnp.clip(jnp.exp(jax.random.uniform(seeds[12], (WIDTH,), jnp.float32, math.log(0.1), math.log(1.0))), 0.1, 1.0),
        "head_gain": jnp.clip(1.0 + 0.1 * jax.random.normal(seeds[13], (WIDTH,), jnp.float32), 0.5, 1.5),
        "head_bias": scatter_about(seeds[14], (WIDTH,), 0.5, 3.0, (), jnp.float32),
        "w_proj": scatter_about(seeds[15], (WIDTH, EMBED), WIDTH ** -0.5, 0.109375),
    }


def unit_rows(matrix):
    values = matrix.astype(jnp.float32)
    length = jnp.sqrt(lax.optimization_barrier(jnp.sum(values * values, axis=1, keepdims=True)) + 1e-06)
    return (values / length, length)

def back_unit(gradient, unit_part, length):
    inner_prod = lax.optimization_barrier(jnp.sum(unit_part * gradient, axis=1, keepdims=True))
    return (gradient - unit_part * inner_prod) / length

def pair_tile(images, image_ids, text_rows, text_ids, temper, offset):
    scores = jnp.dot(images, text_rows.T, preferred_element_type=jnp.float32)
    logits = temper * scores + offset
    labels = jnp.where(image_ids[:, None] == text_ids[None, :], 1.0, -1.0)
    weights = (temper * -labels * jax.nn.sigmoid(-labels * logits)).astype(jnp.bfloat16)
    image_part = jnp.dot(weights, text_rows, preferred_element_type=jnp.float32)
    text_part = jnp.dot(weights.T, images, preferred_element_type=jnp.float32)
    return (image_part, text_part)

def depthwise(pictures, kernel):
    reach = KERNEL // 2
    padded = jnp.pad(pictures, ((0, 0), (reach, reach), (reach, reach), (0, 0)))
    summed = jnp.zeros_like(pictures)
    for above in range(KERNEL):
        for across in range(KERNEL):
            summed = summed + kernel[above * KERNEL + across] * padded[:, above:above + SIDE, across:across + SIDE, :]
    return summed

def layer_norm(values, gain_vec, bias_vec):
    centre = lax.optimization_barrier(jnp.mean(values, axis=-1, keepdims=True))
    centred = values - centre
    inverse = 1.0 / jnp.sqrt(lax.optimization_barrier(jnp.mean(centred * centred, axis=-1, keepdims=True)) + 1e-06)
    normal = centred * inverse
    return (normal * gain_vec + bias_vec, normal, inverse)

def head_back(patch_means, block_mean, image_sum, layer_scale, head_gain, head_bias, w_proj):
    pooled = patch_means.astype(jnp.float32) + layer_scale * block_mean
    head_out, head_norm, inverse = layer_norm(pooled, head_gain, head_bias)
    embed = jnp.dot(head_out.astype(jnp.bfloat16), w_proj, preferred_element_type=jnp.float32)
    embed_unit, embed_len = unit_rows(embed)
    embed_grad = back_unit(image_sum, embed_unit, embed_len).astype(jnp.bfloat16)
    head_grad = jnp.dot(embed_grad, w_proj.T, preferred_element_type=jnp.float32)
    norm_grad = head_grad * head_gain
    pool_grad = inverse * (norm_grad - lax.optimization_barrier(jnp.mean(norm_grad, axis=1, keepdims=True)) - head_norm * lax.optimization_barrier(jnp.mean(norm_grad * head_norm, axis=1, keepdims=True)))
    return (layer_scale * pool_grad / (SIDE * SIDE)).astype(jnp.bfloat16)

def reference(img_emb, txt_emb, img_ids, txt_ids, temp_log, logit_bias, block_in, dw_kernel, ln_gain, ln_bias, w_up, w_down, layer_scale, head_gain, head_bias, w_proj):
    temper = jnp.exp(temp_log[0])
    offset = logit_bias[0]
    img_unit, img_len = unit_rows(img_emb)
    txt_unit, txt_len = unit_rows(txt_emb)
    img_b = img_unit.astype(jnp.bfloat16)
    txt_b = txt_unit.astype(jnp.bfloat16)
    group_rows = N_FSDP * PAIR_DEV
    col_rows = N_DP * PAIR_DEV
    txt_cols = txt_b.reshape(N_DP, N_FSDP, PAIR_DEV, EMBED)
    id_cols = txt_ids.reshape(N_DP, N_FSDP, PAIR_DEV)

    def tile(running, tile_no):
        img_tot, txt_tot = running
        group_no = tile_no // N_FSDP
        column_no = tile_no % N_FSDP
        images = lax.dynamic_slice_in_dim(img_b, group_no * group_rows, group_rows, 0)
        image_ids = lax.dynamic_slice_in_dim(img_ids, group_no * group_rows, group_rows, 0)
        text_rows = lax.dynamic_index_in_dim(txt_cols, column_no, 1, keepdims=False).reshape(col_rows, EMBED)
        text_ids = lax.dynamic_index_in_dim(id_cols, column_no, 1, keepdims=False).reshape(col_rows)
        image_part, text_part = pair_tile(images, image_ids, text_rows, text_ids, temper, offset)
        image_part = lax.optimization_barrier(image_part.astype(jnp.bfloat16)).astype(jnp.float32)
        text_part = lax.optimization_barrier(text_part.astype(jnp.bfloat16)).astype(jnp.float32)
        return ((img_tot.at[group_no].add(image_part), txt_tot.at[column_no].add(text_part)), None)
    start = (jnp.zeros((N_DP, group_rows, EMBED), jnp.float32), jnp.zeros((N_FSDP, col_rows, EMBED), jnp.float32))
    (img_tot, txt_tot), _ = lax.scan(tile, start, jnp.arange(N_DP * N_FSDP, dtype=jnp.int32))
    img_sum = img_tot.reshape(PAIRS, EMBED)
    txt_sum = jnp.transpose(txt_tot.reshape(N_FSDP, N_DP, PAIR_DEV, EMBED), (1, 0, 2, 3)).reshape(PAIRS, EMBED)
    img_grad = back_unit(img_sum, img_unit, img_len)
    txt_grad = back_unit(txt_sum, txt_unit, txt_len)
    patch_rows = N_FSDP * SIDE * SIDE
    down_wide = w_down.astype(jnp.float32)

    def group_step(running, group_no):
        up_tot, down_tot = running
        patches = lax.dynamic_slice_in_dim(block_in, group_no * patch_rows, patch_rows, 0).astype(jnp.float32)
        pictures = patches.reshape(N_FSDP, SIDE, SIDE, WIDTH)
        mixed_rows = depthwise(pictures, dw_kernel).reshape(patch_rows, WIDTH)
        normed = layer_norm(mixed_rows, ln_gain, ln_bias)[0].astype(jnp.bfloat16)
        hidden = jnp.dot(normed, w_up, preferred_element_type=jnp.float32)
        active = jax.nn.gelu(hidden).astype(jnp.bfloat16)
        active_mean = lax.optimization_barrier(jnp.mean(active.astype(jnp.float32).reshape(N_FSDP, SIDE * SIDE, HIDDEN_SIZE), axis=1))
        block_mean = jnp.dot(active_mean, down_wide, precision=lax.Precision.HIGHEST)
        patch_means = lax.optimization_barrier(jnp.mean(pictures, axis=(1, 2))).astype(jnp.bfloat16)
        group_sum = lax.dynamic_slice_in_dim(img_sum, group_no * group_rows, group_rows, 0)
        micro_sum = group_sum.reshape(N_FSDP, PAIR_DEV, EMBED)[:, 0]
        grad_row = head_back(patch_means, block_mean, micro_sum, layer_scale, head_gain, head_bias, w_proj)
        out_grad = jnp.broadcast_to(grad_row[:, None, :], (N_FSDP, SIDE * SIDE, WIDTH)).reshape(patch_rows, WIDTH)
        down_grad = jnp.dot(out_grad, w_down.T, preferred_element_type=jnp.float32)
        _, pullback = jax.vjp(jax.nn.gelu, hidden)
        hid_grad = pullback(down_grad)[0].astype(jnp.bfloat16)
        down_part = jnp.dot(active.T, out_grad, preferred_element_type=jnp.float32)
        up_part = jnp.dot(normed.T, hid_grad, preferred_element_type=jnp.float32)
        up_tot = up_tot + lax.optimization_barrier(up_part.astype(jnp.bfloat16)).astype(jnp.float32)
        down_tot = down_tot + lax.optimization_barrier(down_part.astype(jnp.bfloat16)).astype(jnp.float32)
        return ((up_tot, down_tot), None)
    start = (jnp.zeros((WIDTH, HIDDEN_SIZE), jnp.float32), jnp.zeros((HIDDEN_SIZE, WIDTH), jnp.float32))
    (w_up_grad, w_down_grad), _ = lax.scan(group_step, start, jnp.arange(N_DP, dtype=jnp.int32))
    return (img_grad, txt_grad, w_up_grad, w_down_grad)
```

```python
import jax
import jax.numpy as jnp
from jax import lax
from jax.sharding import PartitionSpec as P

KERNEL = 7
SIDE = 8


def unit_rows(matrix):
    values = matrix.astype(jnp.float32)
    length = jnp.sqrt(jnp.sum(values * values, axis=1, keepdims=True) + 1e-06)
    return (values / length, length)


def back_unit(gradient, unit_part, length):
    inner_prod = jnp.sum(unit_part * gradient, axis=1, keepdims=True)
    return (gradient - unit_part * inner_prod) / length


def depthwise(pictures, kernel):
    reach = KERNEL // 2
    padded = jnp.pad(pictures, ((0, 0), (reach, reach), (reach, reach), (0, 0)))
    summed = jnp.zeros_like(pictures)
    for above in range(KERNEL):
        for across in range(KERNEL):
            summed = (
                summed
                + kernel[above * KERNEL + across]
                * padded[:, above : above + SIDE, across : across + SIDE, :]
            )
    return summed


def layer_norm(values, gain_vec, bias_vec):
    centre = jnp.mean(values, axis=-1, keepdims=True)
    centred = values - centre
    inverse = 1.0 / jnp.sqrt(jnp.mean(centred * centred, axis=-1, keepdims=True) + 1e-06)
    normal = centred * inverse
    return (normal * gain_vec + bias_vec, normal, inverse)


def head_back(patch_means, block_mean, image_sum, layer_scale, head_gain, head_bias, w_proj):
    pooled = patch_means.astype(jnp.float32) + layer_scale * block_mean
    head_out, head_norm, inverse = layer_norm(pooled, head_gain, head_bias)
    embed = jnp.dot(head_out.astype(jnp.bfloat16), w_proj, preferred_element_type=jnp.float32)
    embed_unit, embed_len = unit_rows(embed)
    embed_grad = back_unit(image_sum, embed_unit, embed_len).astype(jnp.bfloat16)
    head_grad = jnp.dot(embed_grad, w_proj.T, preferred_element_type=jnp.float32)
    norm_grad = head_grad * head_gain
    pool_grad = inverse * (
        norm_grad
        - jnp.mean(norm_grad, axis=1, keepdims=True)
        - head_norm * jnp.mean(norm_grad * head_norm, axis=1, keepdims=True)
    )
    return (layer_scale * pool_grad / (SIDE * SIDE)).astype(jnp.bfloat16)


def id_columns(ids):
    codes = jnp.stack([ids // 256, ids % 256], axis=1).astype(jnp.bfloat16)
    return jnp.pad(codes, ((0, 0), (0, 126)))


def split_two(values):
    high = lax.reduce_precision(values, 8, 7)
    low = values - high
    return high.astype(jnp.bfloat16), low.astype(jnp.bfloat16)


def pair_tile_coded(images, image_codes, text_rows, text_codes, temper, offset):
    scores = jnp.dot(images, text_rows.T, preferred_element_type=jnp.float32)
    logits = temper * scores + offset
    same = (image_codes[:, 0][:, None] == text_codes[:, 0][None, :]) & (
        image_codes[:, 1][:, None] == text_codes[:, 1][None, :]
    )
    labels = jnp.where(same, 1.0, -1.0)
    weights = (temper * -labels * jax.nn.sigmoid(-labels * logits)).astype(jnp.bfloat16)
    image_part = jnp.dot(weights, text_rows, preferred_element_type=jnp.float32)
    text_part = jnp.dot(weights.T, images, preferred_element_type=jnp.float32)
    return (image_part, text_part)


def on_device(
    img_emb,
    txt_emb,
    img_ids,
    txt_ids,
    temp_log,
    logit_bias,
    block_in,
    dw_kernel,
    ln_gain,
    ln_bias,
    w_up,
    w_down,
    layer_scale,
    head_gain,
    head_bias,
    w_proj,
):
    channels = block_in.shape[1]
    hid_width = w_up.shape[1]
    embed_width = img_emb.shape[1]
    pairs = img_emb.shape[0]
    patches = SIDE * SIDE
    n_dp, n_fsdp = lax.axis_size("dp"), lax.axis_size("fsdp")
    temper = jnp.exp(temp_log[0])
    offset = logit_bias[0]
    img_unit, img_len = unit_rows(img_emb)
    txt_unit, txt_len = unit_rows(txt_emb)
    img_b = jnp.concatenate([img_unit.astype(jnp.bfloat16), id_columns(img_ids)], axis=1)
    txt_b = jnp.concatenate([txt_unit.astype(jnp.bfloat16), id_columns(txt_ids)], axis=1)
    group_img = lax.all_gather(img_b, "fsdp", axis=0, tiled=True)
    column_txt = lax.all_gather(txt_b, "dp", axis=0, tiled=True)
    pictures = block_in.astype(jnp.float32).reshape(1, SIDE, SIDE, channels)
    mixed_rows = depthwise(pictures, dw_kernel).reshape(patches, channels)
    normed = layer_norm(mixed_rows, ln_gain, ln_bias)[0].astype(jnp.bfloat16)
    patch_means = jnp.mean(pictures, axis=(1, 2)).astype(jnp.bfloat16)
    group_normed = lax.all_gather(normed, "fsdp", axis=0, tiled=True)
    image_part, text_part = pair_tile_coded(
        group_img[:, :embed_width],
        group_img[:, embed_width:],
        column_txt[:, :embed_width],
        column_txt[:, embed_width:],
        temper,
        offset,
    )
    hidden = jnp.dot(group_normed, w_up, preferred_element_type=jnp.float32)
    activated, pullback = jax.vjp(jax.nn.gelu, hidden)
    slope = pullback(jnp.ones_like(hidden))[0].astype(jnp.bfloat16)
    active_total = jnp.sum(
        activated.astype(jnp.bfloat16).astype(jnp.float32).reshape(n_fsdp, patches, hid_width),
        axis=1,
    )
    high, low = split_two(active_total / patches)
    both = jnp.dot(jnp.concatenate([high, low]), w_down, preferred_element_type=jnp.float32)
    partial_mean = both[:n_fsdp] + both[n_fsdp:]
    mean_rows = channels // embed_width
    fill = -(pairs + mean_rows) % 16
    terms = jnp.concatenate(
        [
            image_part.astype(jnp.bfloat16).reshape(n_fsdp, pairs, embed_width),
            partial_mean.astype(jnp.bfloat16).reshape(n_fsdp, mean_rows, embed_width),
            jnp.zeros((n_fsdp, fill, embed_width), jnp.bfloat16),
        ],
        axis=1,
    ).reshape(-1, embed_width)
    term_sum = lax.psum_scatter(terms, "fsdp", scatter_dimension=0, tiled=True).astype(jnp.float32)
    image_sum = term_sum[:pairs]
    block_mean = term_sum[pairs : pairs + mean_rows].reshape(1, channels)
    all_slope = lax.all_gather(slope, "dp", axis=0, tiled=True)
    own_normed = lax.all_to_all(group_normed, "dp", split_axis=1, concat_axis=0, tiled=True)
    all_active = lax.all_gather(active_total, "dp", axis=0, tiled=True)
    grad_row = head_back(
        patch_means, block_mean, image_sum[:1], layer_scale, head_gain, head_bias, w_proj
    )
    all_grad = lax.all_gather(grad_row, ("dp", "fsdp"), axis=0, tiled=True)
    row_down = jnp.dot(all_grad, w_down.T, preferred_element_type=jnp.float32)
    hid_grad = (
        (all_slope.reshape(n_dp * n_fsdp, patches, hid_width).astype(jnp.float32) * row_down[:, None, :])
        .astype(jnp.bfloat16)
        .reshape(-1, hid_width)
    )
    w_up_grad = lax.dot_general(
        own_normed, hid_grad, (((0,), (0,)), ((), ())), preferred_element_type=jnp.float32
    )
    share = channels // n_dp
    own_grad = lax.dynamic_slice_in_dim(all_grad, lax.axis_index("dp") * share, share, 1)
    high, low = split_two(all_active)
    w_down_grad = lax.dot_general(
        jnp.concatenate([high, low]),
        jnp.concatenate([own_grad, own_grad]),
        (((0,), (0,)), ((), ())),
        preferred_element_type=jnp.float32,
    )
    text_sum = lax.psum_scatter(
        text_part.astype(jnp.bfloat16), "dp", scatter_dimension=0, tiled=True
    ).astype(jnp.float32)
    img_grad = back_unit(image_sum, img_unit, img_len)
    txt_grad = back_unit(text_sum, txt_unit, txt_len)
    return (img_grad, txt_grad, w_up_grad, w_down_grad)


def solution(mesh):
    in_specs = (
        P(("dp", "fsdp"), None),
        P(("dp", "fsdp"), None),
        P(("dp", "fsdp")),
        P(("dp", "fsdp")),
        P(),
        P(),
        P(("dp", "fsdp"), None),
        P(),
        P(),
        P(),
        P(None, "fsdp"),
        P("fsdp", None),
        P(),
        P(),
        P(),
        P(),
    )
    out_specs = (P(("dp", "fsdp"), None), P(("dp", "fsdp"), None), P("dp", "fsdp"), P("fsdp", "dp"))
    return jax.shard_map(
        on_device, mesh=mesh, in_specs=in_specs, out_specs=out_specs, check_vma=False
    )
```

```python
import functools

import jax
import jax.numpy as jnp
from jax import lax
from jax.experimental import pallas as pl
from jax.experimental.pallas import tpu as pltpu
from jax.sharding import PartitionSpec as P

KERNEL = 7
SIDE = 8


def unit_rows(matrix):
    values = matrix.astype(jnp.float32)
    length = jnp.sqrt(jnp.sum(values * values, axis=1, keepdims=True) + 1e-06)
    return (values / length, length)


def back_unit(gradient, unit_part, length):
    inner_prod = jnp.sum(unit_part * gradient, axis=1, keepdims=True)
    return (gradient - unit_part * inner_prod) / length


def depthwise(pictures, kernel):
    reach = KERNEL // 2
    padded = jnp.pad(pictures, ((0, 0), (reach, reach), (reach, reach), (0, 0)))
    summed = jnp.zeros_like(pictures)
    for above in range(KERNEL):
        for across in range(KERNEL):
            summed = (
                summed
                + kernel[above * KERNEL + across]
                * padded[:, above : above + SIDE, across : across + SIDE, :]
            )
    return summed


def layer_norm(values, gain_vec, bias_vec):
    centre = jnp.mean(values, axis=-1, keepdims=True)
    centred = values - centre
    inverse = 1.0 / jnp.sqrt(jnp.mean(centred * centred, axis=-1, keepdims=True) + 1e-06)
    normal = centred * inverse
    return (normal * gain_vec + bias_vec, normal, inverse)


MESH = pl.DeviceIdType.MESH
VMEM = pl.BlockSpec(memory_space=pltpu.VMEM)
ANY = pl.BlockSpec(memory_space=pl.ANY)


def greet_peers(n_dp, n_fsdp):
    d, f = lax.axis_index("dp"), lax.axis_index("fsdp")
    barrier = pltpu.get_barrier_semaphore()
    for k in range(1, n_dp):
        pl.semaphore_signal(barrier, inc=1, device_id={"dp": (d + k) % n_dp}, device_id_type=MESH)
    for k in range(1, n_fsdp):
        pl.semaphore_signal(barrier, inc=1, device_id={"fsdp": (f + k) % n_fsdp}, device_id_type=MESH)
    pl.semaphore_wait(barrier, n_dp + n_fsdp - 2)


def push(source, target, send_sem, recv_sem, **peer):
    return pltpu.make_async_remote_copy(
        src_ref=source,
        dst_ref=target,
        send_sem=send_sem,
        recv_sem=recv_sem,
        device_id=peer,
        device_id_type=MESH,
    )


def first_kernel(n_dp, n_fsdp, spread, norm, img, txt, grp, gimg, ctxt, own, *sems):
    loc, txt_s, txt_r, img_s, img_r, rgt_s, rgt_r, lft_s, lft_r, col_s, col_r, col_l = sems
    d, f = lax.axis_index("dp"), lax.axis_index("fsdp")
    share = norm.shape[1] // n_dp
    keep = [
        pltpu.make_async_copy(norm, grp.at[f], loc.at[0]),
        pltpu.make_async_copy(img, gimg.at[f], loc.at[1]),
        pltpu.make_async_copy(txt, ctxt.at[d], loc.at[2]),
    ]
    for copy in keep:
        copy.start()
    greet_peers(n_dp, n_fsdp)

    def right(h, source, b):
        return push(source, grp.at[b], rgt_s.at[h], rgt_r.at[h], fsdp=f + 1)

    def left(h, source, b):
        return push(source, grp.at[b], lft_s.at[h], lft_r.at[h], fsdp=f - 1)

    def columns(source, owner):
        return source.at[:, pl.ds(pl.multiple_of(owner * share, 128), share)]

    def column_copy(k, source, b):
        peer = (d + k) % n_dp
        return push(columns(source, peer), own.at[d, b], col_s.at[b, k - 1], col_r.at[b, k - 1], dp=peer)

    def scatter(source, b):
        if spread:
            for k in range(1, n_dp):
                column_copy(k, source, b).start()
            pltpu.make_async_copy(columns(source, d), own.at[d, b], col_l.at[b]).start()

    @pl.when(f < n_fsdp - 1)
    def _():
        right(0, norm, f).start()

    @pl.when(f > 0)
    def _():
        left(0, norm, f).start()

    pushes = []
    for k in range(1, n_fsdp):
        pushes.append(push(img, gimg.at[f], img_s.at[k - 1], img_r.at[k - 1], fsdp=(f + k) % n_fsdp))
    for k in range(1, n_dp):
        pushes.append(push(txt, ctxt.at[d], txt_s.at[k - 1], txt_r.at[k - 1], dp=(d + k) % n_dp))
    for copy in pushes:
        copy.start()
    scatter(norm, f)

    for h in range(1, n_fsdp):

        @pl.when(f - h >= 0)
        def _():
            b = f - h
            right(h - 1, norm, b).wait_recv()

            @pl.when(f < n_fsdp - 1)
            def _():
                right(h, grp.at[b], b).start()

            scatter(grp.at[b], b)

        @pl.when(f + h <= n_fsdp - 1)
        def _():
            b = f + h
            left(h - 1, norm, b).wait_recv()

            @pl.when(f > 0)
            def _():
                left(h, grp.at[b], b).start()

            scatter(grp.at[b], b)

    for h in range(n_fsdp - 1):

        @pl.when((f - h >= 0) & (f < n_fsdp - 1))
        def _():
            right(h, norm, f - h).wait_send()

        @pl.when((f + h <= n_fsdp - 1) & (f > 0))
        def _():
            left(h, norm, f + h).wait_send()

    for copy in pushes:
        copy.wait()
    for copy in keep:
        copy.wait()
    if spread:
        for b in range(n_fsdp):
            for k in range(1, n_dp):
                column_copy(k, norm, b).wait()
            pltpu.make_async_copy(columns(norm, d), own.at[d, b], col_l.at[b]).wait()


def gather_first(n_dp, n_fsdp, normed, img_b, txt_b):
    rows, channels = normed.shape
    share = channels // n_dp
    spread = share % 128 == 0
    dma = pltpu.SemaphoreType.DMA
    kind = normed.dtype
    return pl.pallas_call(
        functools.partial(first_kernel, n_dp, n_fsdp, spread),
        out_shape=(
            jax.ShapeDtypeStruct((n_fsdp, rows, channels), kind),
            jax.ShapeDtypeStruct((n_fsdp, *img_b.shape), kind),
            jax.ShapeDtypeStruct((n_dp, *txt_b.shape), kind),
            jax.ShapeDtypeStruct((n_dp, n_fsdp, rows, share), kind),
        ),
        in_specs=[VMEM] * 3,
        out_specs=(VMEM,) * 4,
        scratch_shapes=[dma((3,))]
        + [dma((n_dp - 1,))] * 2
        + [dma((n_fsdp - 1,))] * 2
        + [dma((n_fsdp,))] * 4
        + [dma((n_fsdp, n_dp - 1))] * 2
        + [dma((n_fsdp,))],
        compiler_params=pltpu.CompilerParams(
            collective_id=0, has_side_effects=True, vmem_limit_bytes=40 << 20
        ),
    )(normed, img_b, txt_b)


def second_kernel(
    n_dp, n_fsdp, slope, crit, imgs, txts, act, means, scale, gain, bias, proj_hbm,
    all_slope, all_grad, all_act, img_sum, txt_sum,
    proj, crit_in, imgs_in, txts_in, lines, *sems,
):
    loc, slo_s, slo_r, fwd_s, fwd_r, cri_s, cri_r, ims_s, ims_r, txs_s, txs_r, act_s, act_r, gra_s, gra_r, grd_s, grd_r = sems
    d, f = lax.axis_index("dp"), lax.axis_index("fsdp")
    embed_width, channels = proj.shape[1], proj.shape[0]
    keep = [
        pltpu.make_async_copy(proj_hbm, proj, loc.at[0]),
        pltpu.make_async_copy(slope, all_slope.at[d], loc.at[1]),
        pltpu.make_async_copy(act, all_act.at[d], loc.at[2]),
    ]
    for copy in keep:
        copy.start()
    greet_peers(n_dp, n_fsdp)
    critical, late, blocks, passed = [], [], [], []
    for k in range(1, n_fsdp):
        peer = (f + k) % n_fsdp
        critical.append(push(crit.at[peer], crit_in.at[k - 1], cri_s.at[k - 1], cri_r.at[k - 1], fsdp=peer))
        late.append(push(imgs.at[peer], imgs_in.at[k - 1], ims_s.at[k - 1], ims_r.at[k - 1], fsdp=peer))
    partner = d + 1 - 2 * (d % 2)
    for k in range(2, n_dp, 2):
        blocks.append(push(slope, all_slope.at[d], slo_s.at[k // 2], slo_r.at[k // 2], dp=(d + k) % n_dp))
        source = (d + n_dp - k) % n_dp
        passed.append(push(all_slope.at[source], all_slope.at[source], fwd_s.at[k // 2], fwd_r.at[k // 2], dp=partner))
    near = push(slope, all_slope.at[d], slo_s.at[0], slo_r.at[0], dp=partner)
    for k in range(1, n_dp):
        peer = (d + k) % n_dp
        late.append(push(txts.at[peer], txts_in.at[k - 1], txs_s.at[k - 1], txs_r.at[k - 1], dp=peer))
        late.append(push(act, all_act.at[d], act_s.at[k - 1], act_r.at[k - 1], dp=peer))
    for copy in critical + blocks + [near] + late:
        copy.start()

    for copy in critical:
        copy.wait()
    total = crit[f].astype(jnp.float32)
    for k in range(1, n_fsdp):
        total = total + crit_in[k - 1].astype(jnp.float32)
    lines[...] = total
    image_row = lines[0:1, :]
    block_mean = jnp.concatenate(
        [lines[i + 1 : i + 2, :] for i in range(channels // embed_width)], axis=1
    )
    pooled = means[...] + scale[...] * block_mean
    centred = pooled - jnp.mean(pooled, axis=1, keepdims=True)
    inverse = 1.0 / jnp.sqrt(jnp.mean(centred * centred, axis=1, keepdims=True) + 1e-06)
    head_norm = centred * inverse
    head_out = head_norm * gain[...] + bias[...]
    keep[0].wait()
    embed = jnp.dot(
        jnp.broadcast_to(head_out, (16, channels)).astype(jnp.bfloat16),
        proj[...],
        preferred_element_type=jnp.float32,
    )[0:1]
    embed_len = jnp.sqrt(jnp.sum(embed * embed, axis=1, keepdims=True) + 1e-06)
    embed_unit = embed / embed_len
    inner_prod = jnp.sum(embed_unit * image_row, axis=1, keepdims=True)
    embed_grad = (image_row - embed_unit * inner_prod) / embed_len
    head_grad = lax.dot_general(
        jnp.broadcast_to(embed_grad, (16, embed_width)).astype(jnp.bfloat16),
        proj[...],
        (((1,), (1,)), ((), ())),
        preferred_element_type=jnp.float32,
    )[0:1]
    norm_grad = head_grad * gain[...]
    pool_grad = inverse * (
        norm_grad
        - jnp.mean(norm_grad, axis=1, keepdims=True)
        - head_norm * jnp.mean(norm_grad * head_norm, axis=1, keepdims=True)
    )
    row = (scale[...] * pool_grad / (SIDE * SIDE)).astype(jnp.bfloat16).astype(jnp.float32)
    for i in range(channels // 128):
        all_grad[d, f, i : i + 1, :] = row[:, i * 128 : (i + 1) * 128]
    grads = []
    for k in range(1, n_fsdp):
        grads.append(push(all_grad.at[d, f], all_grad.at[d, f], gra_s.at[k - 1], gra_r.at[k - 1], fsdp=(f + k) % n_fsdp))
    for copy in grads:
        copy.start()
    for copy in grads:
        copy.wait()
    group_grads = []
    for k in range(1, n_dp):
        group_grads.append(push(all_grad.at[d], all_grad.at[d], grd_s.at[k - 1], grd_r.at[k - 1], dp=(d + k) % n_dp))
    for copy in group_grads:
        copy.start()

    for copy, onward in zip(blocks, passed):
        copy.wait_recv()
        onward.start()
    for copy in late:
        copy.wait()
    total = imgs[f].astype(jnp.float32)
    for k in range(1, n_fsdp):
        total = total + imgs_in[k - 1].astype(jnp.float32)
    img_sum[...] = total
    total = txts[d].astype(jnp.float32)
    for k in range(1, n_dp):
        total = total + txts_in[k - 1].astype(jnp.float32)
    txt_sum[...] = total
    for copy in blocks:
        copy.wait_send()
    for copy in passed + [near] + group_grads + keep[1:]:
        copy.wait()


def exchange_second(n_dp, n_fsdp, slope, crit, imgs, txts, act, means, scale, gain, bias, w_proj):
    channels, embed_width = w_proj.shape
    dma = pltpu.SemaphoreType.DMA
    f32 = jnp.float32
    pairs = imgs.shape[1]
    return pl.pallas_call(
        functools.partial(second_kernel, n_dp, n_fsdp),
        out_shape=(
            jax.ShapeDtypeStruct((n_dp, *slope.shape), slope.dtype),
            jax.ShapeDtypeStruct((n_dp, n_fsdp, channels // 128, 128), f32),
            jax.ShapeDtypeStruct((n_dp, *act.shape), f32),
            jax.ShapeDtypeStruct((pairs, embed_width), f32),
            jax.ShapeDtypeStruct((pairs, embed_width), f32),
        ),
        in_specs=[VMEM] * 9 + [ANY],
        out_specs=(ANY, VMEM, VMEM, VMEM, VMEM),
        scratch_shapes=[
            pltpu.VMEM(w_proj.shape, w_proj.dtype),
            pltpu.VMEM((n_fsdp - 1, *crit.shape[1:]), crit.dtype),
            pltpu.VMEM((n_fsdp - 1, *imgs.shape[1:]), imgs.dtype),
            pltpu.VMEM((n_dp - 1, *txts.shape[1:]), txts.dtype),
            pltpu.VMEM(crit.shape[1:], f32),
            dma((3,)),
        ]
        + [dma((n_dp // 2,))] * 4
        + [dma((n_fsdp - 1,))] * 4
        + [dma((n_dp - 1,))] * 4
        + [dma((n_fsdp - 1,))] * 2
        + [dma((n_dp - 1,))] * 2,
        compiler_params=pltpu.CompilerParams(
            collective_id=1, has_side_effects=True, vmem_limit_bytes=40 << 20
        ),
    )(slope, crit, imgs, txts, act, means, scale, gain, bias, w_proj)


def id_columns(ids):
    codes = jnp.stack([ids // 256, ids % 256], axis=1).astype(jnp.bfloat16)
    return jnp.pad(codes, ((0, 0), (0, 126)))


def split_two(values):
    high = lax.reduce_precision(values, 8, 7)
    low = values - high
    return high.astype(jnp.bfloat16), low.astype(jnp.bfloat16)


def pair_tile_coded(images, image_codes, text_rows, text_codes, temper, offset):
    scores = jnp.dot(images, text_rows.T, preferred_element_type=jnp.float32)
    logits = temper * scores + offset
    same = (image_codes[:, 0][:, None] == text_codes[:, 0][None, :]) & (
        image_codes[:, 1][:, None] == text_codes[:, 1][None, :]
    )
    labels = jnp.where(same, 1.0, -1.0)
    weights = (temper * -labels * jax.nn.sigmoid(-labels * logits)).astype(jnp.bfloat16)
    image_part = jnp.dot(weights, text_rows, preferred_element_type=jnp.float32)
    text_part = jnp.dot(weights.T, images, preferred_element_type=jnp.float32)
    return (image_part, text_part)


def on_device(
    img_emb,
    txt_emb,
    img_ids,
    txt_ids,
    temp_log,
    logit_bias,
    block_in,
    dw_kernel,
    ln_gain,
    ln_bias,
    w_up,
    w_down,
    layer_scale,
    head_gain,
    head_bias,
    w_proj,
):
    channels = block_in.shape[1]
    hid_width = w_up.shape[1]
    embed_width = img_emb.shape[1]
    pairs = img_emb.shape[0]
    patches = SIDE * SIDE
    n_dp, n_fsdp = lax.axis_size("dp"), lax.axis_size("fsdp")
    temper = jnp.exp(temp_log[0])
    offset = logit_bias[0]
    img_unit, img_len = unit_rows(img_emb)
    txt_unit, txt_len = unit_rows(txt_emb)
    img_b = jnp.concatenate([img_unit.astype(jnp.bfloat16), id_columns(img_ids)], axis=1)
    txt_b = jnp.concatenate([txt_unit.astype(jnp.bfloat16), id_columns(txt_ids)], axis=1)
    pictures = block_in.astype(jnp.float32).reshape(1, SIDE, SIDE, channels)
    mixed_rows = depthwise(pictures, dw_kernel).reshape(patches, channels)
    normed = layer_norm(mixed_rows, ln_gain, ln_bias)[0].astype(jnp.bfloat16)
    patch_means = jnp.mean(pictures, axis=(1, 2)).astype(jnp.bfloat16)
    group_blocks, group_img, column_txt, own_normed = gather_first(n_dp, n_fsdp, normed, img_b, txt_b)
    group_normed = group_blocks.reshape(-1, channels)
    group_img = group_img.reshape(n_fsdp * pairs, -1)
    column_txt = column_txt.reshape(n_dp * pairs, -1)
    share = channels // n_dp
    if share % 128 == 0:
        own_normed = own_normed.reshape(-1, share)
    else:
        own_normed = lax.all_to_all(group_normed, "dp", split_axis=1, concat_axis=0, tiled=True)
    image_part, text_part = pair_tile_coded(
        group_img[:, :embed_width],
        group_img[:, embed_width:],
        column_txt[:, :embed_width],
        column_txt[:, embed_width:],
        temper,
        offset,
    )
    hidden = jnp.dot(group_normed, w_up, preferred_element_type=jnp.float32)
    activated, pullback = jax.vjp(jax.nn.gelu, hidden)
    slope = pullback(jnp.ones_like(hidden))[0].astype(jnp.bfloat16)
    active_total = jnp.sum(
        activated.astype(jnp.bfloat16).astype(jnp.float32).reshape(n_fsdp, patches, hid_width),
        axis=1,
    )
    high, low = split_two(active_total / patches)
    both = jnp.dot(jnp.concatenate([high, low]), w_down, preferred_element_type=jnp.float32)
    partial_mean = both[:n_fsdp] + both[n_fsdp:]
    mean_rows = channels // embed_width
    image_terms = image_part.astype(jnp.bfloat16).reshape(n_fsdp, pairs, embed_width)
    crit = jnp.concatenate(
        [
            image_terms[:, :1],
            partial_mean.astype(jnp.bfloat16).reshape(n_fsdp, mean_rows, embed_width),
            jnp.zeros((n_fsdp, -(1 + mean_rows) % 16, embed_width), jnp.bfloat16),
        ],
        axis=1,
    )
    all_slope, all_grad, all_active, image_sum, text_sum = exchange_second(
        n_dp,
        n_fsdp,
        slope,
        crit,
        image_terms,
        text_part.astype(jnp.bfloat16).reshape(n_dp, pairs, embed_width),
        active_total,
        patch_means.astype(jnp.float32).reshape(1, channels),
        layer_scale[None],
        head_gain[None],
        head_bias[None],
        w_proj,
    )
    all_grad = all_grad.reshape(n_dp * n_fsdp, channels).astype(jnp.bfloat16)
    all_active = all_active.reshape(n_dp * n_fsdp, hid_width)
    row_down = jnp.dot(all_grad, w_down.T, preferred_element_type=jnp.float32)
    hid_grad = (
        (all_slope.reshape(n_dp * n_fsdp, patches, hid_width).astype(jnp.float32) * row_down[:, None, :])
        .astype(jnp.bfloat16)
        .reshape(-1, hid_width)
    )
    w_up_grad = lax.dot_general(
        own_normed, hid_grad, (((0,), (0,)), ((), ())), preferred_element_type=jnp.float32
    )
    own_grad = lax.dynamic_slice_in_dim(all_grad, lax.axis_index("dp") * share, share, 1)
    high, low = split_two(all_active)
    w_down_grad = lax.dot_general(
        jnp.concatenate([high, low]),
        jnp.concatenate([own_grad, own_grad]),
        (((0,), (0,)), ((), ())),
        preferred_element_type=jnp.float32,
    )
    img_grad = back_unit(image_sum, img_unit, img_len)
    txt_grad = back_unit(text_sum, txt_unit, txt_len)
    return (img_grad, txt_grad, w_up_grad, w_down_grad)


def solution(mesh):
    in_specs = (
        P(("dp", "fsdp"), None),
        P(("dp", "fsdp"), None),
        P(("dp", "fsdp")),
        P(("dp", "fsdp")),
        P(),
        P(),
        P(("dp", "fsdp"), None),
        P(),
        P(),
        P(),
        P(None, "fsdp"),
        P("fsdp", None),
        P(),
        P(),
        P(),
        P(),
    )
    out_specs = (P(("dp", "fsdp"), None), P(("dp", "fsdp"), None), P("dp", "fsdp"), P("fsdp", "dp"))
    return jax.shard_map(
        on_device, mesh=mesh, in_specs=in_specs, out_specs=out_specs, check_vma=False
    )
```

```python
import functools

import jax
import jax.numpy as jnp
from jax import lax
from jax.experimental import pallas as pl
from jax.experimental.pallas import tpu as pltpu
from jax.sharding import PartitionSpec as P

KERNEL = 7
SIDE = 8


def unit_rows(matrix):
    values = matrix.astype(jnp.float32)
    length = jnp.sqrt(jnp.sum(values * values, axis=1, keepdims=True) + 1e-06)
    return (values / length, length)


def back_unit(gradient, unit_part, length):
    inner_prod = jnp.sum(unit_part * gradient, axis=1, keepdims=True)
    return (gradient - unit_part * inner_prod) / length


def depthwise(pictures, kernel):
    reach = KERNEL // 2
    padded = jnp.pad(pictures, ((0, 0), (reach, reach), (reach, reach), (0, 0)))
    summed = jnp.zeros_like(pictures)
    for above in range(KERNEL):
        for across in range(KERNEL):
            summed = (
                summed
                + kernel[above * KERNEL + across]
                * padded[:, above : above + SIDE, across : across + SIDE, :]
            )
    return summed


def layer_norm(values, gain_vec, bias_vec):
    centre = jnp.mean(values, axis=-1, keepdims=True)
    centred = values - centre
    inverse = 1.0 / jnp.sqrt(jnp.mean(centred * centred, axis=-1, keepdims=True) + 1e-06)
    normal = centred * inverse
    return (normal * gain_vec + bias_vec, normal, inverse)


MESH = pl.DeviceIdType.MESH
VMEM = pl.BlockSpec(memory_space=pltpu.VMEM)
ANY = pl.BlockSpec(memory_space=pl.ANY)


def greet_peers(n_dp, n_fsdp):
    d, f = lax.axis_index("dp"), lax.axis_index("fsdp")
    barrier = pltpu.get_barrier_semaphore()
    for k in range(1, n_dp):
        pl.semaphore_signal(barrier, inc=1, device_id={"dp": (d + k) % n_dp}, device_id_type=MESH)
    for k in range(1, n_fsdp):
        pl.semaphore_signal(barrier, inc=1, device_id={"fsdp": (f + k) % n_fsdp}, device_id_type=MESH)
    pl.semaphore_wait(barrier, n_dp + n_fsdp - 2)


def push(source, target, send_sem, recv_sem, **peer):
    return pltpu.make_async_remote_copy(
        src_ref=source,
        dst_ref=target,
        send_sem=send_sem,
        recv_sem=recv_sem,
        device_id=peer,
        device_id_type=MESH,
    )


def second_parts(x):
    cubic = 0.044715
    slant = 0.7978845608028654
    square = x * x
    t = jnp.tanh(slant * x * (1.0 + cubic * square))
    half = 0.5 * (1.0 + t)
    slope = half + 0.5 * x * (1.0 - t * t) * slant * (1.0 + 3.0 * cubic * square)
    return x * half, slope


def nt_dot(left, right):
    return lax.dot_general(
        left, right, (((1,), (1,)), ((), ())), preferred_element_type=jnp.float32
    )


def whole_kernel(
    n_dp, n_fsdp, spread, norm, img, txt, temper, offset, means, scale, gain, bias,
    up_hbm, down_hbm, proj_hbm,
    grp, own, all_slope, all_grad, all_act, img_sum, txt_sum,
    up, down, proj, gimg, ctxt, slope, crit, imgs, txts, crit_in, imgs_in, txts_in, lines, partial,
    *sems,
):
    (
        loc, txt_s, txt_r, img_s, img_r, rgt_s, rgt_r, lft_s, lft_r, col_s, col_r, col_l,
        slo_l, slo_s, slo_r, fwd_s, fwd_r, cri_s, cri_r, ims_s, ims_r, txs_s, txs_r,
        act_s, act_r, gra_s, gra_r, grd_s, grd_r,
    ) = sems
    d, f = lax.axis_index("dp"), lax.axis_index("fsdp")
    rows, channels = norm.shape
    share = channels // n_dp
    embed_width = proj.shape[1]
    hid_width = up.shape[1]
    pairs = img.shape[0]
    partner = d + 1 - 2 * (d % 2)
    keep = [
        pltpu.make_async_copy(up_hbm, up, loc.at[0]),
        pltpu.make_async_copy(norm, grp.at[f], loc.at[1]),
        pltpu.make_async_copy(img, gimg.at[f], loc.at[2]),
        pltpu.make_async_copy(txt, ctxt.at[d], loc.at[3]),
        pltpu.make_async_copy(down_hbm, down, loc.at[4]),
        pltpu.make_async_copy(proj_hbm, proj, loc.at[5]),
    ]
    for copy in keep:
        copy.start()
    greet_peers(n_dp, n_fsdp)

    def right(h, source, b):
        return push(source, grp.at[b], rgt_s.at[h], rgt_r.at[h], fsdp=f + 1)

    def left(h, source, b):
        return push(source, grp.at[b], lft_s.at[h], lft_r.at[h], fsdp=f - 1)

    def columns(source, owner):
        return source.at[:, pl.ds(pl.multiple_of(owner * share, 128), share)]

    def column_copy(k, source, b):
        peer = (d + k) % n_dp
        return push(columns(source, peer), own.at[d, b], col_s.at[b, k - 1], col_r.at[b, k - 1], dp=peer)

    def scatter(source, b):
        if spread:
            for k in range(1, n_dp):
                column_copy(k, source, b).start()
            pltpu.make_async_copy(columns(source, d), own.at[d, b], col_l.at[b]).start()

    def slope_copy(k, b):
        peer = partner if k == 0 else (d + k) % n_dp
        return push(slope.at[b], all_slope.at[d, b], slo_s.at[b, k // 2], slo_r.at[b, k // 2], dp=peer)

    def slope_keep(b):
        return pltpu.make_async_copy(slope.at[b], all_slope.at[d, b], slo_l.at[b])

    def onward(k, b):
        spot = all_slope.at[(d + n_dp - k) % n_dp, b]
        return push(spot, spot, fwd_s.at[b, k // 2], fwd_r.at[b, k // 2], dp=partner)

    wide = 256 if hid_width % 256 == 0 else 128

    def expand(source, b):
        def tile(i, carry):
            cols = pl.ds(pl.multiple_of(i * wide, wide), wide)
            hidden = jnp.dot(source[...], up[:, cols], preferred_element_type=jnp.float32)
            active, slant = second_parts(hidden)
            slope[b, :, cols] = slant.astype(jnp.bfloat16)
            active = active.astype(jnp.bfloat16).astype(jnp.float32)
            all_act[d, b, :, cols] = jnp.sum(active, axis=0, keepdims=True)
            return carry

        lax.fori_loop(0, hid_width // wide, tile, 0)
        for k in range(0, n_dp, 2):
            slope_copy(k, b).start()
        slope_keep(b).start()

    @pl.when(f < n_fsdp - 1)
    def _():
        right(0, norm, f).start()

    @pl.when(f > 0)
    def _():
        left(0, norm, f).start()

    img_pushes, txt_pushes = [], []
    for k in range(1, n_fsdp):
        img_pushes.append(push(img, gimg.at[f], img_s.at[k - 1], img_r.at[k - 1], fsdp=(f + k) % n_fsdp))
    for k in range(1, n_dp):
        txt_pushes.append(push(txt, ctxt.at[d], txt_s.at[k - 1], txt_r.at[k - 1], dp=(d + k) % n_dp))
    for copy in img_pushes + txt_pushes:
        copy.start()
    scatter(norm, f)
    keep[0].wait()
    expand(norm, f)

    for copy in keep[2:4] + img_pushes + txt_pushes:
        copy.wait()
    images = gimg[...].reshape(n_fsdp * pairs, -1)
    texts = ctxt[...].reshape(n_dp * pairs, -1)
    image_rows, image_codes = images[:, :embed_width], images[:, embed_width:]
    text_rows, text_codes = texts[:, :embed_width], texts[:, embed_width:]

    def weigh(left_rows, left_codes, right_rows, right_codes):
        logits = temper[...] * nt_dot(left_rows, right_rows) + offset[...]
        labels = jnp.where(nt_dot(left_codes, right_codes) == 0.0, 1.0, -1.0)
        return (temper[...] * -labels * jax.nn.sigmoid(-labels * logits)).astype(jnp.bfloat16)

    weights = weigh(image_rows, image_codes, text_rows, text_codes)
    image_part = jnp.dot(weights, text_rows, preferred_element_type=jnp.float32)
    crit[...] = jnp.zeros_like(crit)
    for p in range(n_fsdp):
        imgs[p] = image_part[p * pairs : (p + 1) * pairs].astype(jnp.bfloat16)
        crit[p, 0:1, :] = image_part[p * pairs : p * pairs + 1]
    weights = weigh(text_rows, text_codes, image_rows, image_codes)
    text_part = jnp.dot(weights, image_rows, preferred_element_type=jnp.float32)
    for p in range(n_dp):
        txts[p] = text_part[p * pairs : (p + 1) * pairs].astype(jnp.bfloat16)

    for h in range(1, n_fsdp):

        @pl.when(f - h >= 0)
        def _():
            b = f - h
            right(h - 1, norm, b).wait_recv()

            @pl.when(f < n_fsdp - 1)
            def _():
                right(h, grp.at[b], b).start()

            scatter(grp.at[b], b)

        @pl.when(f + h <= n_fsdp - 1)
        def _():
            b = f + h
            left(h - 1, norm, b).wait_recv()

            @pl.when(f > 0)
            def _():
                left(h, grp.at[b], b).start()

            scatter(grp.at[b], b)

        @pl.when(f - h >= 0)
        def _():
            expand(grp.at[f - h], f - h)

        @pl.when(f + h <= n_fsdp - 1)
        def _():
            expand(grp.at[f + h], f + h)

    critical, late = [], []
    for k in range(1, n_fsdp):
        peer = (f + k) % n_fsdp
        critical.append(push(crit.at[peer], crit_in.at[k - 1], cri_s.at[k - 1], cri_r.at[k - 1], fsdp=peer))
        late.append(push(imgs.at[peer], imgs_in.at[k - 1], ims_s.at[k - 1], ims_r.at[k - 1], fsdp=peer))
    for k in range(1, n_dp):
        peer = (d + k) % n_dp
        late.append(push(all_act.at[d], all_act.at[d], act_s.at[k - 1], act_r.at[k - 1], dp=peer))
        late.append(push(txts.at[peer], txts_in.at[k - 1], txs_s.at[k - 1], txs_r.at[k - 1], dp=peer))

    totals = jnp.concatenate([all_act[d, b] for b in range(n_fsdp)], axis=0) / (SIDE * SIDE)
    high = totals.astype(jnp.bfloat16)
    low = (totals - high.astype(jnp.float32)).astype(jnp.bfloat16)
    both = jnp.concatenate([high.astype(jnp.float32), low.astype(jnp.float32)], axis=0).astype(jnp.bfloat16)
    keep[4].wait()

    def mean_tile(i, carry):
        cols = pl.ds(pl.multiple_of(i * 256, 256), 256)
        product = jnp.dot(both, down[:, cols], preferred_element_type=jnp.float32)
        partial[:, cols] = product[:n_fsdp] + product[n_fsdp:]
        return carry

    lax.fori_loop(0, channels // 256, mean_tile, 0)
    for p in range(n_fsdp):
        for i in range(channels // embed_width):
            crit[p, i + 1 : i + 2, :] = partial[p : p + 1, i * embed_width : (i + 1) * embed_width]
    for copy in critical + late:
        copy.start()
    for copy in critical:
        copy.wait()
    total = crit[f]
    for k in range(1, n_fsdp):
        total = total + crit_in[k - 1]
    lines[...] = total
    image_row = lines[0:1, :]
    block_mean = jnp.concatenate(
        [lines[i + 1 : i + 2, :] for i in range(channels // embed_width)], axis=1
    )
    pooled = means[...] + scale[...] * block_mean
    centred = pooled - jnp.mean(pooled, axis=1, keepdims=True)
    inverse = 1.0 / jnp.sqrt(jnp.mean(centred * centred, axis=1, keepdims=True) + 1e-06)
    head_norm = centred * inverse
    head_out = head_norm * gain[...] + bias[...]
    keep[5].wait()
    embed = jnp.dot(
        jnp.broadcast_to(head_out, (16, channels)).astype(jnp.bfloat16),
        proj[...],
        preferred_element_type=jnp.float32,
    )[0:1]
    embed_len = jnp.sqrt(jnp.sum(embed * embed, axis=1, keepdims=True) + 1e-06)
    embed_unit = embed / embed_len
    inner_prod = jnp.sum(embed_unit * image_row, axis=1, keepdims=True)
    embed_grad = (image_row - embed_unit * inner_prod) / embed_len
    head_grad = lax.dot_general(
        jnp.broadcast_to(embed_grad, (16, embed_width)).astype(jnp.bfloat16),
        proj[...],
        (((1,), (1,)), ((), ())),
        preferred_element_type=jnp.float32,
    )[0:1]
    norm_grad = head_grad * gain[...]
    pool_grad = inverse * (
        norm_grad
        - jnp.mean(norm_grad, axis=1, keepdims=True)
        - head_norm * jnp.mean(norm_grad * head_norm, axis=1, keepdims=True)
    )
    row = (scale[...] * pool_grad / (SIDE * SIDE)).astype(jnp.bfloat16).astype(jnp.float32)
    for i in range(channels // 128):
        all_grad[d, f, i : i + 1, :] = row[:, i * 128 : (i + 1) * 128]
    grads = []
    for k in range(1, n_fsdp):
        grads.append(push(all_grad.at[d, f], all_grad.at[d, f], gra_s.at[k - 1], gra_r.at[k - 1], fsdp=(f + k) % n_fsdp))
    for copy in grads:
        copy.start()
    for copy in grads:
        copy.wait()
    group_grads = []
    for k in range(1, n_dp):
        group_grads.append(push(all_grad.at[d], all_grad.at[d], grd_s.at[k - 1], grd_r.at[k - 1], dp=(d + k) % n_dp))
    for copy in group_grads:
        copy.start()

    for b in range(n_fsdp):
        for k in range(2, n_dp, 2):
            slope_copy(k, b).wait_recv()
            onward(k, b).start()
    for copy in late:
        copy.wait()
    total = imgs[f].astype(jnp.float32)
    for k in range(1, n_fsdp):
        total = total + imgs_in[k - 1].astype(jnp.float32)
    img_sum[...] = total
    total = txts[d].astype(jnp.float32)
    for k in range(1, n_dp):
        total = total + txts_in[k - 1].astype(jnp.float32)
    txt_sum[...] = total
    keep[1].wait()
    for copy in group_grads:
        copy.wait()
    for h in range(n_fsdp - 1):

        @pl.when((f - h >= 0) & (f < n_fsdp - 1))
        def _():
            right(h, norm, f - h).wait_send()

        @pl.when((f + h <= n_fsdp - 1) & (f > 0))
        def _():
            left(h, norm, f + h).wait_send()

    for b in range(n_fsdp):
        slope_copy(0, b).wait()
        slope_keep(b).wait()
        for k in range(2, n_dp, 2):
            slope_copy(k, b).wait_send()
            onward(k, b).wait()
        if spread:
            for k in range(1, n_dp):
                column_copy(k, norm, b).wait()
            pltpu.make_async_copy(columns(norm, d), own.at[d, b], col_l.at[b]).wait()


def run_whole(n_dp, n_fsdp, normed, img_b, txt_b, temper, offset, means, scale, gain, bias, w_up, w_down, w_proj):
    channels, embed_width = w_proj.shape
    rows = normed.shape[0]
    hid_width = w_up.shape[1]
    pairs = img_b.shape[0]
    share = channels // n_dp
    dma = pltpu.SemaphoreType.DMA
    f32, half = jnp.float32, normed.dtype
    shape = jax.ShapeDtypeStruct
    lines = -(-(1 + channels // embed_width) // 8) * 8
    return pl.pallas_call(
        functools.partial(whole_kernel, n_dp, n_fsdp, share % 128 == 0),
        out_shape=(
            shape((n_fsdp, rows, channels), half),
            shape((n_dp, n_fsdp, rows, share), half),
            shape((n_dp, n_fsdp, rows, hid_width), half),
            shape((n_dp, n_fsdp, channels // 128, 128), f32),
            shape((n_dp, n_fsdp, 1, hid_width), f32),
            shape((pairs, embed_width), f32),
            shape((pairs, embed_width), f32),
        ),
        in_specs=[VMEM] * 9 + [ANY] * 3,
        out_specs=(VMEM, VMEM, ANY, VMEM, VMEM, VMEM, VMEM),
        scratch_shapes=[
            pltpu.VMEM(w_up.shape, half),
            pltpu.VMEM(w_down.shape, half),
            pltpu.VMEM(w_proj.shape, half),
            pltpu.VMEM((n_fsdp, *img_b.shape), half),
            pltpu.VMEM((n_dp, *txt_b.shape), half),
            pltpu.VMEM((n_fsdp, rows, hid_width), half),
            pltpu.VMEM((n_fsdp, lines, embed_width), f32),
            pltpu.VMEM((n_fsdp, pairs, embed_width), half),
            pltpu.VMEM((n_dp, pairs, embed_width), half),
            pltpu.VMEM((n_fsdp - 1, lines, embed_width), f32),
            pltpu.VMEM((n_fsdp - 1, pairs, embed_width), half),
            pltpu.VMEM((n_dp - 1, pairs, embed_width), half),
            pltpu.VMEM((lines, embed_width), f32),
            pltpu.VMEM((n_fsdp, channels), f32),
            dma((6,)),
        ]
        + [dma((n_dp - 1,))] * 2
        + [dma((n_fsdp - 1,))] * 2
        + [dma((n_fsdp,))] * 4
        + [dma((n_fsdp, n_dp - 1))] * 2
        + [dma((n_fsdp,))] * 2
        + [dma((n_fsdp, n_dp // 2))] * 4
        + [dma((n_fsdp - 1,))] * 4
        + [dma((n_dp - 1,))] * 4
        + [dma((n_fsdp - 1,))] * 2
        + [dma((n_dp - 1,))] * 2,
        compiler_params=pltpu.CompilerParams(
            collective_id=0, has_side_effects=True, vmem_limit_bytes=60 << 20
        ),
    )(normed, img_b, txt_b, temper, offset, means, scale, gain, bias, w_up, w_down, w_proj)


def id_columns(ids, sign, flip):
    high, low, one = sign * 256 * (ids // 256), sign * (ids % 256), jnp.ones_like(ids)
    codes = [one, one, high, low] if flip else [high, low, one, one]
    return jnp.pad(jnp.stack(codes, axis=1).astype(jnp.bfloat16), ((0, 0), (0, 124)))


def split_two(values):
    high = lax.reduce_precision(values, 8, 7)
    low = values - high
    return high.astype(jnp.bfloat16), low.astype(jnp.bfloat16)


def on_device(
    img_emb,
    txt_emb,
    img_ids,
    txt_ids,
    temp_log,
    logit_bias,
    block_in,
    dw_kernel,
    ln_gain,
    ln_bias,
    w_up,
    w_down,
    layer_scale,
    head_gain,
    head_bias,
    w_proj,
):
    channels = block_in.shape[1]
    hid_width = w_up.shape[1]
    patches = SIDE * SIDE
    n_dp, n_fsdp = lax.axis_size("dp"), lax.axis_size("fsdp")
    temper = jnp.exp(temp_log[0])
    offset = logit_bias[0]
    img_unit, img_len = unit_rows(img_emb)
    txt_unit, txt_len = unit_rows(txt_emb)
    img_b = jnp.concatenate([img_unit.astype(jnp.bfloat16), id_columns(img_ids, 1, False)], axis=1)
    txt_b = jnp.concatenate([txt_unit.astype(jnp.bfloat16), id_columns(txt_ids, -1, True)], axis=1)
    pictures = block_in.astype(jnp.float32).reshape(1, SIDE, SIDE, channels)
    mixed_rows = depthwise(pictures, dw_kernel).reshape(patches, channels)
    normed = layer_norm(mixed_rows, ln_gain, ln_bias)[0].astype(jnp.bfloat16)
    patch_means = jnp.mean(pictures, axis=(1, 2)).astype(jnp.bfloat16)
    group_blocks, own_normed, all_slope, all_grad, all_active, image_sum, text_sum = run_whole(
        n_dp,
        n_fsdp,
        normed,
        img_b,
        txt_b,
        temper.reshape(1, 1),
        offset.reshape(1, 1),
        patch_means.astype(jnp.float32).reshape(1, channels),
        layer_scale[None],
        head_gain[None],
        head_bias[None],
        w_up,
        w_down,
        w_proj,
    )
    group_normed = group_blocks.reshape(-1, channels)
    share = channels // n_dp
    if share % 128 == 0:
        own_normed = own_normed.reshape(-1, share)
    else:
        own_normed = lax.all_to_all(group_normed, "dp", split_axis=1, concat_axis=0, tiled=True)
    all_grad = all_grad.reshape(n_dp * n_fsdp, channels).astype(jnp.bfloat16)
    all_active = all_active.reshape(n_dp * n_fsdp, hid_width)
    row_down = jnp.dot(all_grad, w_down.T, preferred_element_type=jnp.float32)
    hid_grad = (
        (all_slope.reshape(n_dp * n_fsdp, patches, hid_width).astype(jnp.float32) * row_down[:, None, :])
        .astype(jnp.bfloat16)
        .reshape(-1, hid_width)
    )
    w_up_grad = lax.dot_general(
        own_normed, hid_grad, (((0,), (0,)), ((), ())), preferred_element_type=jnp.float32
    )
    own_grad = lax.dynamic_slice_in_dim(all_grad, lax.axis_index("dp") * share, share, 1)
    high, low = split_two(all_active)
    w_down_grad = lax.dot_general(
        jnp.concatenate([high, low]),
        jnp.concatenate([own_grad, own_grad]),
        (((0,), (0,)), ((), ())),
        preferred_element_type=jnp.float32,
    )
    img_grad = back_unit(image_sum, img_unit, img_len)
    txt_grad = back_unit(text_sum, txt_unit, txt_len)
    return (img_grad, txt_grad, w_up_grad, w_down_grad)


def solution(mesh):
    in_specs = (
        P(("dp", "fsdp"), None),
        P(("dp", "fsdp"), None),
        P(("dp", "fsdp")),
        P(("dp", "fsdp")),
        P(),
        P(),
        P(("dp", "fsdp"), None),
        P(),
        P(),
        P(),
        P(None, "fsdp"),
        P("fsdp", None),
        P(),
        P(),
        P(),
        P(),
    )
    out_specs = (P(("dp", "fsdp"), None), P(("dp", "fsdp"), None), P("dp", "fsdp"), P("fsdp", "dp"))
    return jax.shard_map(
        on_device, mesh=mesh, in_specs=in_specs, out_specs=out_specs, check_vma=False
    )
```
